256 devices in a mesh: seq: 64 (over z, x, core), tensor: 4 (over y).
Axes of the slice: x: 4, y: 4, z: 8, core: 2. Of those that a mesh axis runs over, the one named last changes fastest.
Arguments:
- acts: bfloat16 [32768, 28672], P('seq', 'tensor'), may hold values from -6 to 6
- out_grads: bfloat16 [32768, 8192], P('seq', 'tensor'), may hold values from -6 to 6
- proj_in: bfloat16 [28672, 64], P('tensor'), may hold values from -0.03125 to 0.03125
- proj_out: bfloat16 [8192, 64], P('tensor'), may hold values from -0.0625 to 0.0625
- prior_cov: float32 [4096, 4096], P('seq', 'tensor'), may hold values from -0.2 to 0.2, as said below
Outputs:
- covariance: float32 [4096, 4096], P('seq', 'tensor')
The draws below stay inside these ranges and needn't reach their ends.
Inputs may be any that keep to these rules, and one draw needn't show every extreme that they name: `prior_cov`: symmetric.
All inputs are finite; a program needn't handle non-finite values.
Results may differ from the reference program's by a relative error of at most 0.0003.
Values sent between devices are 32-bit elements; how exact they have to be, the bound alone decides.
A program may use at most 64 MiB of HBM per device.

```python
import jax
import jax.numpy as jnp
from jax import lax

D = 8192
FF = 28672
RANK = 64
LEN = 256
SEQS = 128
TOKENS = 32768


def draw_prior_cov(key, part):
    matrix_order = RANK * RANK
    base = 0.05 * jax.random.normal(key, (matrix_order, matrix_order), jnp.float32)
    symmetric = (base + base.T) * 0.7071
    return jnp.clip(symmetric, -0.2, 0.2)


def block_scale(own_key, shape, shards, smallest, top_value):
    def one(axis_at, blocks):
        draws = jax.random.uniform(jax.random.fold_in(jax.random.fold_in(own_key, 6), axis_at), (blocks,), jnp.float32, smallest / len(shards), top_value / len(shards))
        return jnp.repeat(jnp.exp(draws), shape[axis_at] // blocks).reshape((-1,) + (1,) * (len(shape) - axis_at - 1))

    factor_of = one(*shards[0])
    for cut in shards[1:]:
        factor_of = factor_of * one(*cut)
    return factor_of


def normal_values(rng, dims, deviation, reach, split=(), held_as=jnp.bfloat16):
    result = deviation * jax.random.normal(rng, dims, jnp.float32)
    if split:
        result = result * block_scale(rng, dims, split, -0.22, 0.18)
    return jnp.clip(result, -reach, reach).astype(held_as)


def setup_inputs(seed: int = 0) -> dict:
    arg_keys = jax.random.split(jax.random.key(seed), 6)
    return {
        "acts": normal_values(arg_keys[0], (TOKENS, FF), 1.0, 6.0, ((0, 64), (1, 4))),
        "out_grads": normal_values(arg_keys[1], (TOKENS, D), 1.0, 6.0, ((0, 64), (1, 4))),
        "proj_in": normal_values(arg_keys[2], (FF, RANK), FF ** -0.5, 0.03125, ((0, 4),)),
        "proj_out": normal_values(arg_keys[3], (D, RANK), D ** -0.5, 0.0625, ((0, 4),)),
        "prior_cov": draw_prior_cov(jax.random.fold_in(arg_keys[5], 71), 0),
    }


def reference(acts, out_grads, proj_in, proj_out, prior_cov):
    seq_acts = acts.reshape(SEQS, LEN, FF)
    seq_grads = out_grads.reshape(SEQS, LEN, D)

    def one_sequence(pair):
        act_rows, grad_rows = pair
        in_proj = jnp.dot(act_rows, proj_in, preferred_element_type=jnp.float32)
        out_proj = jnp.dot(grad_rows, proj_out, preferred_element_type=jnp.float32)
        outer = jnp.einsum('lo,li->oi', out_proj, in_proj, precision=lax.Precision.HIGHEST)
        return (outer / jnp.sqrt(jnp.float32(LEN))).reshape(RANK * RANK)
    grads_ex = lax.map(one_sequence, (seq_acts, seq_grads))
    gram = jnp.dot(grads_ex.T, grads_ex, precision=lax.Precision.HIGHEST)
    return prior_cov + gram / jnp.float32(SEQS)
```

```python
import functools

import jax
import jax.numpy as jnp
from jax import lax
from jax.experimental import pallas as pl
from jax.experimental.pallas import tpu as pltpu
from jax.sharding import PartitionSpec as P

RANK = 64
LEN = 256
NZ, NX, NK, NC = 8, 4, 2, 4
MESH = pl.DeviceIdType.MESH
BF = jnp.bfloat16
F32 = jnp.float32
STOP = 9


def split(v):
    hi = v.astype(BF)
    return hi, (v - hi.astype(F32)).astype(BF)


def dot_t(a, b):
    return lax.dot_general(a, b, (((1,), (1,)), ((), ())), preferred_element_type=F32)


def dot(a, b):
    return lax.dot_general(a, b, (((1,), (0,)), ((), ())), preferred_element_type=F32)


def kernel(
    acts, grads, pin, pout, prior, out,
    a_v, g_v, pi_v, po_v, prior_v, part, rsbuf, tmp, pbuf, sbuf, rowl, rowz, rowt, rowbuf, colbuf,
    ld_sem, w_sem, rs_s, rs_r, p_s, p_r, z_s, z_r, zr_s, zr_r, x_s, x_r, c_s, c_r, r2_s, r2_r,
):
    r = lax.axis_index("seq")
    c = lax.axis_index("tensor")
    z = r // (NX * NK)
    x = (r // NK) % NX
    k = r % NK

    def seq_of(zz, xx, kk):
        return (zz * NX + xx) * NK + kk

    tok = acts.shape[0] // NC
    order = (2, 1, 3, 0)

    weights = [
        pltpu.make_async_copy(pin, pi_v, w_sem.at[0]),
        pltpu.make_async_copy(pout, po_v, w_sem.at[1]),
    ]
    prior_copy = pltpu.make_async_copy(prior, prior_v, w_sem.at[2])
    loads = []
    for n, dc in enumerate(order):
        rows = pl.ds(pl.multiple_of(((c + dc) % NC) * tok, tok), tok)
        loads.append(
            (
                pltpu.make_async_copy(acts.at[rows], a_v.at[n], ld_sem.at[n, 0]),
                pltpu.make_async_copy(grads.at[rows], g_v.at[n], ld_sem.at[n, 1]),
            )
        )
    weights[0].start()
    weights[1].start()
    for pair in loads:
        pair[0].start()
        pair[1].start()
    prior_copy.start()

    barrier = pltpu.get_barrier_semaphore()
    peers = [(r, (c + d) % NC) for d in range(1, NC)]
    peers += [(seq_of((z + d) % NZ, x, k), c) for d in range(1, NZ)]
    peers += [(seq_of(z, (x + d) % NX, kk), c) for d in range(1, NX) for kk in range(NK)]
    peers += [(seq_of(z, x, 1 - k), c)]
    for peer in peers:
        pl.semaphore_signal(barrier, inc=1, device_id=peer, device_id_type=MESH)

    def remote(src, dst, s, rs, peer):
        return pltpu.make_async_remote_copy(
            src_ref=src, dst_ref=dst, send_sem=s, recv_sem=rs, device_id=peer, device_id_type=MESH
        )

    weights[0].wait()
    weights[1].wait()
    sends = []
    for n, dc in enumerate(order):
        loads[n][0].wait()
        loads[n][1].wait()
        inp = dot_t(pi_v[...], a_v[n])
        outp = dot_t(po_v[...], g_v[n])
        if n == 0:
            pl.semaphore_wait(barrier, len(peers))
        if dc == 0:
            rsbuf[c, :RANK] = inp
            rsbuf[c, RANK:] = outp
        else:
            part[n, :RANK] = inp
            part[n, RANK:] = outp
            copy = remote(part.at[n], rsbuf.at[c], rs_s.at[dc], rs_r.at[dc], (r, (c + dc) % NC))
            copy.start()
            sends.append(copy)
    if STOP <= 1:
        for copy in sends:
            copy.wait()
        prior_copy.wait()
        out[...] = prior_v[...] + rsbuf[0, 0, 0]
        return
    for copy in sends:
        copy.wait_recv()
    both = (rsbuf[0] + rsbuf[1]) + (rsbuf[2] + rsbuf[3])
    hi, lo = split(both)
    in_hi, in_lo = hi[:RANK], lo[:RANK]
    o_hi, o_lo = hi[RANK:], lo[RANK:]
    dup_hi = jnp.concatenate([in_hi, in_hi], axis=0)
    dup_lo = jnp.concatenate([in_lo, in_lo], axis=0)
    tmp[...] = dot_t(o_hi, dup_hi) + (dot_t(o_hi, dup_lo) + dot_t(o_lo, dup_hi))
    half = RANK // 2
    low = lax.broadcasted_iota(jnp.int32, (half, 2 * RANK), 1) < RANK
    pbuf[c] = jnp.where(low, tmp[pl.ds(0, half, stride=2), :], tmp[pl.ds(1, half, stride=2), :])

    p_copies = []
    for dc in (2, 1, 3):
        copy = remote(pbuf.at[c], pbuf.at[c], p_s.at[dc], p_r.at[dc], (r, (c + dc) % NC))
        copy.start()
        p_copies.append(copy)
    for copy in p_copies:
        copy.wait_recv()
    scale = 1.0 / 16.0
    s0 = (pbuf[0] + pbuf[1]) * scale
    s1 = (pbuf[2] + pbuf[3]) * scale
    sbuf[:half] = s0
    sbuf[half:] = s1
    rowl[pl.ds(0, half, stride=2), :] = jnp.where(low, s0, pltpu.roll(s1, RANK, 1))
    rowl[pl.ds(1, half, stride=2), :] = jnp.where(low, pltpu.roll(s0, RANK, 1), s1)

    def piece(xx, kk, zz):
        return pl.ds(pl.multiple_of(((xx * NK + kk) * NZ + zz) * 16, 16), 16)

    def tile(i):
        return pl.ds(pl.multiple_of(i * 8, 8), 8)

    own = pl.multiple_of(((x * NK + k) * NZ + z) * 16, 16)
    colbuf[pl.ds(own, 8), :] = sbuf[tile(c), :]
    colbuf[pl.ds(own + 8, 8), :] = sbuf[tile(c + NC), :]
    rowz[tile(z), :] = rowl[tile(z), :]
    if STOP <= 2:
        for copy in sends + p_copies:
            copy.wait_send()
        prior_copy.wait()
        out[...] = prior_v[...] + colbuf[0, 0]
        return

    def z_col(dz):
        ref = colbuf.at[piece(x, k, z)]
        return remote(ref, ref, z_s, z_r.at[dz], (seq_of((z + dz) % NZ, x, k), c))

    def z_row(dz):
        zz = (z + dz) % NZ
        return remote(rowl.at[tile(zz)], rowz.at[tile(z)], zr_s, zr_r, (seq_of(zz, x, k), c))

    def x_col(dx, dz):
        ref = colbuf.at[piece(x, k, (z - dz) % NZ)]
        return remote(ref, ref, x_s, x_r.at[dx, dz], (seq_of(z, (x + dx) % NX, k), c))

    def c_col(dx, dz):
        ref = colbuf.at[piece((x - dx) % NX, k, (z - dz) % NZ)]
        return remote(ref, ref, c_s, c_r, (seq_of(z, x, 1 - k), c))

    for dz in (4, 3, 5, 2, 6, 1, 7):
        z_row(dz).start()
        z_col(dz).start()

    def have_z(dz):
        if dz:
            z_col(dz).wait_recv()
        for dx in (2, 1, 3):
            x_col(dx, dz).start()
        c_col(0, dz).start()

    def have_x(dx, dz):
        x_col(dx, dz).wait_recv()
        c_col(dx, dz).start()

    have_z(0)
    for dz in (1, 7):
        have_z(dz)
    for dz in (2, 6):
        have_z(dz)
    for dx in (1, 3, 2):
        have_x(dx, 0)
    for dz in (3, 5):
        have_z(dz)
    for dx in (1, 3):
        for dz in (1, 7):
            have_x(dx, dz)
    have_z(4)

    pltpu.make_async_copy(rowz.at[pl.ds(0, 56)], rowz.at[pl.ds(0, 56)], zr_r).wait()
    for j in range(8):
        rowt[8 * j : 8 * j + 8, :] = rowz[pl.ds(j, 8, stride=8), :]
    me = x * NK + k
    rowbuf[tile(me), :] = rowt[tile(me), :]
    for dx in (2, 1, 3, 0):
        for dk in range(NK):
            if dx or dk:
                xx = (x + dx) % NX
                kk = (k + dk) % NK
                remote(
                    rowt.at[tile(xx * NK + kk)], rowbuf.at[tile(me)], r2_s, r2_r, (seq_of(z, xx, kk), c)
                ).start()

    for dz in (1, 7):
        have_x(2, dz)
    for dz in (2, 6, 3, 5, 4):
        for dx in (1, 3, 2):
            have_x(dx, dz)

    pltpu.make_async_copy(rowbuf.at[pl.ds(0, 56)], rowbuf.at[pl.ds(0, 56)], r2_r).wait()
    flipped = rowbuf[...].T
    lhs = jnp.concatenate([flipped[:RANK], flipped[RANK:]], axis=1)
    l_hi, l_lo = split(lhs)
    pltpu.make_async_copy(colbuf.at[pl.ds(0, 512)], colbuf.at[pl.ds(0, 512)], c_r).wait()
    prior_copy.wait()
    for p in range(8):
        block = jnp.concatenate(
            [colbuf[pl.ds(p, 64, stride=16), :], colbuf[pl.ds(8 + p, 64, stride=16), :]], axis=0
        )
        b_hi, b_lo = split(block)
        gram = dot(l_hi, b_hi) + (dot(l_hi, b_lo) + dot(l_lo, b_hi))
        cols = slice(128 * p, 128 * p + 128)
        out[:, cols] = prior_v[:, cols] + gram * (1.0 / 128.0)

    for copy in sends + p_copies:
        copy.wait_send()
    here = (r, c)
    for sem, rows in ((z_s, 112), (x_s, 384), (c_s, 512)):
        ref = colbuf.at[pl.ds(0, rows)]
        pltpu.make_async_copy(ref, ref, sem).wait()
    for sem in (zr_s, r2_s):
        pltpu.make_async_copy(rowz.at[pl.ds(0, 56)], rowz.at[pl.ds(0, 56)], sem).wait()


def per_device(acts, out_grads, proj_in, proj_out, prior_cov):
    tokens, ff = acts.shape
    d = out_grads.shape[1]
    tok = tokens // NC
    hbm = pl.BlockSpec(memory_space=pl.ANY)
    dma = pltpu.SemaphoreType.DMA
    return pl.pallas_call(
        kernel,
        out_shape=jax.ShapeDtypeStruct(prior_cov.shape, F32),
        in_specs=[hbm] * 5,
        out_specs=pl.BlockSpec(memory_space=pltpu.VMEM),
        scratch_shapes=[
            pltpu.VMEM((NC, tok, ff), BF),
            pltpu.VMEM((NC, tok, d), BF),
            pltpu.VMEM((RANK, ff), BF),
            pltpu.VMEM((RANK, d), BF),
            pltpu.VMEM(prior_cov.shape, F32),
            pltpu.VMEM((3, 2 * RANK, tok), F32),
            pltpu.VMEM((NC, 2 * RANK, tok), F32),
            pltpu.VMEM((RANK, 2 * RANK), F32),
            pltpu.VMEM((NC, RANK // 2, 2 * RANK), F32),
            pltpu.VMEM((RANK, 2 * RANK), F32),
            pltpu.VMEM((RANK, 2 * RANK), F32),
            pltpu.VMEM((RANK, 2 * RANK), F32),
            pltpu.VMEM((RANK, 2 * RANK), F32),
            pltpu.VMEM((RANK, 2 * RANK), F32),
            pltpu.VMEM((RANK * 16, 2 * RANK), F32),
            dma((NC, 2)),
            dma((3,)),
            dma((NC,)),
            dma((NC,)),
            dma((NC,)),
            dma((NC,)),
            dma(()),
            dma((NZ,)),
            dma(()),
            dma(()),
            dma(()),
            dma((NX, NZ)),
            dma(()),
            dma(()),
            dma(()),
            dma(()),
        ],
        compiler_params=pltpu.CompilerParams(
            collective_id=0, has_side_effects=True, vmem_limit_bytes=56 * 1024 * 1024
        ),
    )(acts, out_grads, proj_in.T, proj_out.T, prior_cov)


def solution(mesh):
    in_specs = (
        P("seq", "tensor"),
        P("seq", "tensor"),
        P("tensor", None),
        P("tensor", None),
        P("seq", "tensor"),
    )
    return jax.shard_map(
        per_device, mesh=mesh, in_specs=in_specs, out_specs=P("seq", "tensor"), check_vma=False
    )
```

```python
import functools

import jax
import jax.numpy as jnp
from jax import lax
from jax.experimental import pallas as pl
from jax.experimental.pallas import tpu as pltpu
from jax.sharding import PartitionSpec as P

RANK = 64
LEN = 256
NZ, NX, NK, NC = 8, 4, 2, 4
MESH = pl.DeviceIdType.MESH
BF = jnp.bfloat16
F32 = jnp.float32
STOP = 9
CUTS = 1
GROUPS = (2, 1, 3, 0)
MEET = 0
WINDOW = 3


def split(v):
    hi = v.astype(BF)
    return hi, (v - hi.astype(F32)).astype(BF)


def dot_t(a, b):
    return lax.dot_general(a, b, (((1,), (1,)), ((), ())), preferred_element_type=F32)


def dot(a, b):
    return lax.dot_general(a, b, (((1,), (0,)), ((), ())), preferred_element_type=F32)


def kernel(
    acts, grads, pin, pout, prior, out,
    a_v, g_v, pi_v, po_v, prior_v, part, rsbuf, tmp, pbuf, sbuf, rowl, rowbuf, colbuf,
    ld_sem, w_sem, rs_s, rs_r, p_s, p_r, col_s, col_r, row_s, row_r, cc_s, cc_r, cr_s, cr_r, met,
):
    r = lax.axis_index("seq")
    c = lax.axis_index("tensor")
    z = r // (NX * NK)
    x = (r // NK) % NX
    k = r % NK

    def seq_of(zz, xx, kk):
        return (zz * NX + xx) * NK + kk

    tok = acts.shape[0] // NC
    ff = acts.shape[1]
    wide = ff // CUTS
    order = (2, 1, 3, 0)

    weights = [
        pltpu.make_async_copy(pin, pi_v, w_sem.at[0]),
        pltpu.make_async_copy(pout, po_v, w_sem.at[1]),
    ]
    prior_copy = pltpu.make_async_copy(prior, prior_v, w_sem.at[2])
    loads = []
    for n, dc in enumerate(order):
        rows = pl.ds(pl.multiple_of(((c + dc) % NC) * tok, tok), tok)
        for cut in range(CUTS):
            cols = pl.ds(cut * wide, wide)
            loads.append(
                pltpu.make_async_copy(acts.at[rows, cols], a_v.at[n, :, cols], ld_sem.at[n, cut])
            )
        loads.append(pltpu.make_async_copy(grads.at[rows], g_v.at[n], ld_sem.at[n, CUTS]))
    weights[0].start()
    for load in loads[:CUTS]:
        load.start()
    weights[1].start()
    for load in loads[CUTS:WINDOW]:
        load.start()

    barrier = pltpu.get_barrier_semaphore()
    peers = [(r, (c + d) % NC) for d in range(1, NC)]
    peers += [(seq_of(z, x, 1 - k), c)]
    line = {d: (seq_of((z + d) % NZ, x, k), c) for d in (1, 2, NZ - 2, NZ - 1)}
    across = [(seq_of(z, (x + d) % NX, k), c) for d in range(1, NX)]
    peers += [line[1], line[NZ - 1]] + across

    def tell(sem, group):
        for peer in group:
            pl.semaphore_signal(sem, inc=1, device_id=peer, device_id_type=MESH)

    tell(barrier, peers)

    def remote(src, dst, s, rs, peer):
        return pltpu.make_async_remote_copy(
            src_ref=src, dst_ref=dst, send_sem=s, recv_sem=rs, device_id=peer, device_id_type=MESH
        )

    pending = iter(loads[WINDOW:] + [prior_copy])

    def arrived(load):
        load.wait()
        follower = next(pending, None)
        if follower is not None:
            follower.start()

    sends = []
    weights[0].wait()
    for n, dc in enumerate(order):
        inp = None
        for cut in range(CUTS):
            arrived(loads[n * (CUTS + 1) + cut])
            cols = slice(cut * wide, cut * wide + wide)
            term = dot_t(a_v[n, :, cols], pi_v[:, cols])
            inp = term if inp is None else inp + term
        arrived(loads[n * (CUTS + 1) + CUTS])
        if n == 0:
            weights[1].wait()
        outp = dot_t(g_v[n], po_v[...])
        if dc == 0:
            rsbuf[c, :, :RANK] = inp
            rsbuf[c, :, RANK:] = outp
        else:
            part[n, :, :RANK] = inp
            part[n, :, RANK:] = outp
        if n == MEET:
            pl.semaphore_wait(barrier, len(peers))
            tell(met.at[0], [line[1], line[NZ - 1]])
        if n >= MEET:
            for m in range(0 if n == MEET else n, n + 1):
                dm = order[m]
                if dm and STOP > 0:
                    peer = (r, (c + dm) % NC)
                    copy = remote(part.at[m], rsbuf.at[c], rs_s.at[dm], rs_r.at[dm], peer)
                    copy.start()
                    sends.append(copy)
    pl.semaphore_wait(met.at[0], 2)
    tell(met.at[1], [line[2], line[NZ - 2]])
    if STOP <= 1:
        for copy in sends:
            copy.wait()
        prior_copy.wait()
        pl.semaphore_wait(met.at[1], 2)
        out[...] = prior_v[...] + rsbuf[0, 0, 0]
        return
    for copy in sends:
        copy.wait_recv()
    both = ((rsbuf[0] + rsbuf[1]) + (rsbuf[2] + rsbuf[3])).T
    hi, lo = split(both)
    in_hi, in_lo = hi[:RANK], lo[:RANK]
    o_hi, o_lo = hi[RANK:], lo[RANK:]
    dup_hi = jnp.concatenate([in_hi, in_hi], axis=0)
    dup_lo = jnp.concatenate([in_lo, in_lo], axis=0)
    tmp[...] = dot_t(o_hi, dup_hi) + (dot_t(o_hi, dup_lo) + dot_t(o_lo, dup_hi))
    half = RANK // 2
    low = lax.broadcasted_iota(jnp.int32, (half, 2 * RANK), 1) < RANK
    pbuf[c] = jnp.where(low, tmp[pl.ds(0, half, stride=2), :], tmp[pl.ds(1, half, stride=2), :])

    p_copies = []
    for dc in (2, 1, 3):
        copy = remote(pbuf.at[c], pbuf.at[c], p_s.at[dc], p_r.at[dc], (r, (c + dc) % NC))
        copy.start()
        p_copies.append(copy)
    pl.semaphore_wait(met.at[1], 2)
    tell(met.at[2], across)
    for copy in p_copies:
        copy.wait_recv()
    pl.semaphore_wait(met.at[2], NX - 1)
    scale = 1.0 / 16.0
    s0 = (pbuf[0] + pbuf[1]) * scale
    s1 = (pbuf[2] + pbuf[3]) * scale
    sbuf[:half] = s0
    sbuf[half:] = s1
    rowl[:, 0, :] = s0
    rowl[:, 1, :] = s1

    def slot(zz, xx, kk):
        return (kk * NX + xx) * NZ + zz

    def piece(i):
        return colbuf.at[pl.ds(pl.multiple_of(i * 16, 16), 16)]

    def tile(i):
        return pl.ds(pl.multiple_of(i * 8, 8), 8)

    me = slot(z, x, k)
    own = pl.multiple_of(me * 16, 16)
    colbuf[pl.ds(own, 8), :] = sbuf[tile(c), :]
    colbuf[pl.ds(own + 8, 8), :] = sbuf[tile(c + NC), :]
    rowbuf[me] = rowl[z * NX + x]
    if STOP <= 2:
        for copy in sends + p_copies:
            copy.wait_send()
        prior_copy.wait()
        out[...] = prior_v[...] + colbuf[0, 0]
        return

    def col(dz, dx):
        peer = (seq_of((z + dz) % NZ, (x + dx) % NX, k), c)
        return remote(piece(me), piece(me), col_s, col_r.at[dx], peer)

    def row(dz, dx):
        zz, xx = (z + dz) % NZ, (x + dx) % NX
        return remote(rowl.at[zz * NX + xx], rowbuf.at[me], row_s, row_r.at[dx], (seq_of(zz, xx, k), c))

    sibling = (seq_of(z, x, 1 - k), c)

    def col_group(xx, count):
        return colbuf.at[pl.ds(pl.multiple_of(slot(0, xx, k) * 16, 128), count * 16)]

    def row_group(xx, count):
        return rowbuf.at[pl.ds(slot(0, xx, k), count)]

    for dx in GROUPS:
        for dz in (4, 3, 5, 2, 6, 1, 7, 0):
            if dz or dx:
                row(dz, dx).start()
                col(dz, dx).start()
    for dx in GROUPS:
        count = NZ if dx else NZ - 1
        xx = (x - dx) % NX
        for group, arrival, s, rs in ((col_group, col_r, cc_s, cc_r), (row_group, row_r, cr_s, cr_r)):
            got = group(xx, count)
            pltpu.make_async_copy(got, got, arrival.at[dx]).wait()
            whole = group(xx, NZ)
            remote(whole, whole, s, rs, sibling).start()

    total = NZ * NX
    mine = colbuf.at[pl.ds(0, total * 16)]
    mine_rows = rowbuf.at[pl.ds(0, total)]
    pltpu.make_async_copy(mine_rows, mine_rows, cr_r).wait()
    even = (jnp.zeros((NZ * NX * NK, 2 * RANK), jnp.int32) + k) == 0
    parts = []
    for h in range(2):
        v = rowbuf[:, h, :]
        parts.append(jnp.where(even, v, pltpu.roll(v, RANK, 1)))
    lhs = jnp.concatenate(parts, axis=0).T[:RANK]
    l_hi, l_lo = split(lhs)
    prior_copy.wait()
    pltpu.make_async_copy(mine, mine, cc_r).wait()
    for p in range(8):
        block = jnp.concatenate(
            [colbuf[pl.ds(p, 64, stride=16), :], colbuf[pl.ds(8 + p, 64, stride=16), :]], axis=0
        )
        b_hi, b_lo = split(block)
        gram = dot(l_hi, b_hi) + (dot(l_hi, b_lo) + dot(l_lo, b_hi))
        cols = slice(128 * p, 128 * p + 128)
        out[:, cols] = prior_v[:, cols] + gram * (1.0 / 128.0)

    for copy in sends + p_copies:
        copy.wait_send()
    others = colbuf.at[pl.ds(0, (total - 1) * 16)]
    other_rows = rowbuf.at[pl.ds(0, total - 1)]
    pltpu.make_async_copy(others, others, col_s).wait()
    pltpu.make_async_copy(other_rows, other_rows, row_s).wait()
    pltpu.make_async_copy(mine, mine, cc_s).wait()
    pltpu.make_async_copy(mine_rows, mine_rows, cr_s).wait()


def per_device(acts, out_grads, proj_in, proj_out, prior_cov):
    tokens, ff = acts.shape
    d = out_grads.shape[1]
    tok = tokens // NC
    hbm = pl.BlockSpec(memory_space=pl.ANY)
    dma = pltpu.SemaphoreType.DMA
    return pl.pallas_call(
        kernel,
        out_shape=pltpu.VMEM(prior_cov.shape, F32),
        in_specs=[hbm] * 5,
        out_specs=pl.BlockSpec(memory_space=pltpu.VMEM),
        scratch_shapes=[
            pltpu.VMEM((NC, tok, ff), BF),
            pltpu.VMEM((NC, tok, d), BF),
            pltpu.VMEM((RANK, ff), BF),
            pltpu.VMEM((RANK, d), BF),
            pltpu.VMEM(prior_cov.shape, F32),
            pltpu.VMEM((3, tok, 2 * RANK), F32),
            pltpu.VMEM((NC, tok, 2 * RANK), F32),
            pltpu.VMEM((RANK, 2 * RANK), F32),
            pltpu.VMEM((NC, RANK // 2, 2 * RANK), F32),
            pltpu.VMEM((RANK, 2 * RANK), F32),
            pltpu.VMEM((RANK // 2, 2, 2 * RANK), F32),
            pltpu.VMEM((RANK, 2, 2 * RANK), F32),
            pltpu.VMEM((RANK * 16, 2 * RANK), F32),
            dma((NC, CUTS + 1)),
            dma((3,)),
            dma((NC,)),
            dma((NC,)),
            dma((NC,)),
            dma((NC,)),
            dma(()),
            dma((NX,)),
            dma(()),
            dma((NX,)),
            dma(()),
            dma(()),
            dma(()),
            dma(()),
            pltpu.SemaphoreType.REGULAR((3,)),
        ],
        compiler_params=pltpu.CompilerParams(
            collective_id=0, has_side_effects=True, vmem_limit_bytes=56 * 1024 * 1024
        ),
    )(acts, out_grads, proj_in.T, proj_out.T, prior_cov)


def solution(mesh):
    in_specs = (
        P("seq", "tensor"),
        P("seq", "tensor"),
        P("tensor", None),
        P("tensor", None),
        P("seq", "tensor"),
    )
    return jax.shard_map(
        per_device, mesh=mesh, in_specs=in_specs, out_specs=P("seq", "tensor"), check_vma=False
    )
```

```python
import functools

import jax
import jax.numpy as jnp
from jax import lax
from jax.experimental import pallas as pl
from jax.experimental.pallas import tpu as pltpu
from jax.sharding import PartitionSpec as P

RANK = 64
LEN = 256
NZ, NX, NK, NC = 8, 4, 2, 4
MESH = pl.DeviceIdType.MESH
BF = jnp.bfloat16
F32 = jnp.float32
STOP = 9
GROUPS = (2, 1, 3, 0)


def split(v):
    hi = v.astype(BF)
    return hi, (v - hi.astype(F32)).astype(BF)


def dot_t(a, b):
    return lax.dot_general(a, b, (((1,), (1,)), ((), ())), preferred_element_type=F32)


def dot(a, b):
    return lax.dot_general(a, b, (((1,), (0,)), ((), ())), preferred_element_type=F32)


def kernel(
    acts, grads, pin, pout, prior, out,
    a_v, g_v, pi_v, po_v, prior_v, part, rsbuf, tmp, pbuf, sbuf, rowl, rowbuf, colbuf,
    ld_sem, w_sem, rs_s, rs_r, p_s, p_r, col_s, col_r, row_s, row_r, cc_s, cc_r, cr_s, cr_r, met,
):
    r = lax.axis_index("seq")
    c = lax.axis_index("tensor")
    z = r // (NX * NK)
    x = (r // NK) % NX
    k = r % NK

    def seq_of(zz, xx, kk):
        return (zz * NX + xx) * NK + kk

    tok = acts.shape[0] // NC
    weights = [
        pltpu.make_async_copy(pin, pi_v, w_sem.at[0]),
        pltpu.make_async_copy(pout, po_v, w_sem.at[1]),
    ]
    prior_copy = pltpu.make_async_copy(prior, prior_v, w_sem.at[2])

    def shift(n):
        return (2 + 3 * n + 3 * (n * (n - 1) // 2)) % NC

    def rows_of(n):
        return pl.ds(pl.multiple_of(((c + shift(n)) % NC) * tok, tok), tok)

    def load_acts(n):
        return pltpu.make_async_copy(acts.at[rows_of(n)], a_v.at[n], ld_sem.at[n, 0])

    def load_grads(n):
        return pltpu.make_async_copy(grads.at[rows_of(n)], g_v.at[n], ld_sem.at[n, 1])

    weights[0].start()
    load_acts(0).start()
    weights[1].start()
    load_grads(0).start()
    load_acts(1).start()

    barrier = pltpu.get_barrier_semaphore()
    peers = [(r, (c + d) % NC) for d in range(1, NC)]
    peers += [(seq_of(z, x, 1 - k), c)]
    line = {d: (seq_of((z + d) % NZ, x, k), c) for d in (1, 2, NZ - 2, NZ - 1)}
    across = [(seq_of(z, (x + d) % NX, k), c) for d in range(1, NX)]
    peers += [line[1], line[NZ - 1]] + across

    def tell(sem, group):
        for peer in group:
            pl.semaphore_signal(sem, inc=1, device_id=peer, device_id_type=MESH)

    tell(barrier, peers)

    def remote(src, dst, s, rs, peer):
        return pltpu.make_async_remote_copy(
            src_ref=src, dst_ref=dst, send_sem=s, recv_sem=rs, device_id=peer, device_id_type=MESH
        )

    def rs_copy(n):
        dc = shift(n)
        peer = (r, (c + dc) % NC)
        return remote(part.at[n], rsbuf.at[dc], rs_s.at[dc], rs_r.at[dc], peer)

    weights[0].wait()
    weights[1].wait()

    def block(n, carry):
        load_acts(n).wait()

        @pl.when(n < NC - 1)
        def _():
            load_grads(n + 1).start()

        part[n, :, :RANK] = dot_t(a_v[n], pi_v[...])
        load_grads(n).wait()

        @pl.when(n < NC - 2)
        def _():
            load_acts(n + 2).start()

        @pl.when(n == NC - 2)
        def _():
            prior_copy.start()

        part[n, :, RANK:] = dot_t(g_v[n], po_v[...])

        @pl.when(n == 0)
        def _():
            pl.semaphore_wait(barrier, len(peers))
            tell(met.at[0], [line[1], line[NZ - 1]])

        if STOP > 0:

            @pl.when(n < NC - 1)
            def _():
                rs_copy(n).start()

        return carry

    lax.fori_loop(0, NC, block, 0)
    sends = [rs_copy(n) for n in range(NC - 1)] if STOP > 0 else []
    pl.semaphore_wait(met.at[0], 2)
    tell(met.at[1], [line[2], line[NZ - 2]])
    if STOP <= 1:
        for copy in sends:
            copy.wait()
        prior_copy.wait()
        pl.semaphore_wait(met.at[1], 2)
        out[...] = prior_v[...] + rsbuf[0, 0, 0]
        return
    for copy in sends:
        copy.wait_recv()
    both = ((part[3] + rsbuf[2]) + (rsbuf[1] + rsbuf[3])).T
    hi, lo = split(both)
    in_hi, in_lo = hi[:RANK], lo[:RANK]
    o_hi, o_lo = hi[RANK:], lo[RANK:]
    dup_hi = jnp.concatenate([in_hi, in_hi], axis=0)
    dup_lo = jnp.concatenate([in_lo, in_lo], axis=0)
    tmp[...] = dot_t(o_hi, dup_hi) + (dot_t(o_hi, dup_lo) + dot_t(o_lo, dup_hi))
    half = RANK // 2
    low = lax.broadcasted_iota(jnp.int32, (half, 2 * RANK), 1) < RANK
    pbuf[c] = jnp.where(low, tmp[pl.ds(0, half, stride=2), :], tmp[pl.ds(1, half, stride=2), :])

    p_copies = []
    for dc in (2, 1, 3):
        copy = remote(pbuf.at[c], pbuf.at[c], p_s.at[dc], p_r.at[dc], (r, (c + dc) % NC))
        copy.start()
        p_copies.append(copy)
    pl.semaphore_wait(met.at[1], 2)
    tell(met.at[2], across)
    for copy in p_copies:
        copy.wait_recv()
    pl.semaphore_wait(met.at[2], NX - 1)
    scale = 1.0 / 16.0
    s0 = (pbuf[0] + pbuf[1]) * scale
    s1 = (pbuf[2] + pbuf[3]) * scale
    sbuf[:half] = s0
    sbuf[half:] = s1
    rowl[:, 0, :] = s0
    rowl[:, 1, :] = s1

    def slot(zz, xx, kk):
        return (kk * NX + xx) * NZ + zz

    def piece(i):
        return colbuf.at[pl.ds(pl.multiple_of(i * 16, 16), 16)]

    def tile(i):
        return pl.ds(pl.multiple_of(i * 8, 8), 8)

    me = slot(z, x, k)
    own = pl.multiple_of(me * 16, 16)
    colbuf[pl.ds(own, 8), :] = sbuf[tile(c), :]
    colbuf[pl.ds(own + 8, 8), :] = sbuf[tile(c + NC), :]
    rowbuf[me] = rowl[z * NX + x]
    if STOP <= 2:
        for copy in sends + p_copies:
            copy.wait_send()
        prior_copy.wait()
        out[...] = prior_v[...] + colbuf[0, 0]
        return

    def col(dz, dx):
        peer = (seq_of((z + dz) % NZ, (x + dx) % NX, k), c)
        return remote(piece(me), piece(me), col_s, col_r.at[dx], peer)

    def row(dz, dx):
        zz, xx = (z + dz) % NZ, (x + dx) % NX
        return remote(rowl.at[zz * NX + xx], rowbuf.at[me], row_s, row_r.at[dx], (seq_of(zz, xx, k), c))

    sibling = (seq_of(z, x, 1 - k), c)

    def col_group(xx, count):
        return colbuf.at[pl.ds(pl.multiple_of(slot(0, xx, k) * 16, 128), count * 16)]

    def row_group(xx, count):
        return rowbuf.at[pl.ds(slot(0, xx, k), count)]

    def send(t, carry):
        dx, j = shift(t // NZ), t % NZ
        dz = NZ // 2 + (1 - 2 * (j % 2)) * ((j + 1) // 2)
        row(dz, dx).start()
        col(dz, dx).start()
        return carry

    lax.fori_loop(0, NZ * NX - 1, send, 0)
    for dx in GROUPS:
        count = NZ if dx else NZ - 1
        xx = (x - dx) % NX
        for group, arrival, s, rs in ((col_group, col_r, cc_s, cc_r), (row_group, row_r, cr_s, cr_r)):
            got = group(xx, count)
            pltpu.make_async_copy(got, got, arrival.at[dx]).wait()
            whole = group(xx, NZ)
            remote(whole, whole, s, rs, sibling).start()

    total = NZ * NX
    mine = colbuf.at[pl.ds(0, total * 16)]
    mine_rows = rowbuf.at[pl.ds(0, total)]
    pltpu.make_async_copy(mine_rows, mine_rows, cr_r).wait()
    even = (jnp.zeros((NZ * NX * NK, 2 * RANK), jnp.int32) + k) == 0
    parts = []
    for h in range(2):
        v = rowbuf[:, h, :]
        parts.append(jnp.where(even, v, pltpu.roll(v, RANK, 1)))
    lhs = jnp.concatenate(parts, axis=0).T[:RANK]
    l_hi, l_lo = split(lhs)
    prior_copy.wait()
    pltpu.make_async_copy(mine, mine, cc_r).wait()
    for p in range(8):
        block = jnp.concatenate(
            [colbuf[pl.ds(p, 64, stride=16), :], colbuf[pl.ds(8 + p, 64, stride=16), :]], axis=0
        )
        b_hi, b_lo = split(block)
        gram = dot(l_hi, b_hi) + (dot(l_hi, b_lo) + dot(l_lo, b_hi))
        cols = slice(128 * p, 128 * p + 128)
        out[:, cols] = prior_v[:, cols] + gram * (1.0 / 128.0)

    for copy in sends + p_copies:
        copy.wait_send()
    others = colbuf.at[pl.ds(0, (total - 1) * 16)]
    other_rows = rowbuf.at[pl.ds(0, total - 1)]
    pltpu.make_async_copy(others, others, col_s).wait()
    pltpu.make_async_copy(other_rows, other_rows, row_s).wait()
    pltpu.make_async_copy(mine, mine, cc_s).wait()
    pltpu.make_async_copy(mine_rows, mine_rows, cr_s).wait()


def per_device(acts, out_grads, proj_in, proj_out, prior_cov):
    tokens, ff = acts.shape
    d = out_grads.shape[1]
    tok = tokens // NC
    hbm = pl.BlockSpec(memory_space=pl.ANY)
    dma = pltpu.SemaphoreType.DMA
    return pl.pallas_call(
        kernel,
        out_shape=pltpu.VMEM(prior_cov.shape, F32),
        in_specs=[hbm] * 5,
        out_specs=pl.BlockSpec(memory_space=pltpu.VMEM),
        scratch_shapes=[
            pltpu.VMEM((NC, tok, ff), BF),
            pltpu.VMEM((NC, tok, d), BF),
            pltpu.VMEM((RANK, ff), BF),
            pltpu.VMEM((RANK, d), BF),
            pltpu.VMEM(prior_cov.shape, F32),
            pltpu.VMEM((NC, tok, 2 * RANK), F32),
            pltpu.VMEM((NC, tok, 2 * RANK), F32),
            pltpu.VMEM((RANK, 2 * RANK), F32),
            pltpu.VMEM((NC, RANK // 2, 2 * RANK), F32),
            pltpu.VMEM((RANK, 2 * RANK), F32),
            pltpu.VMEM((RANK // 2, 2, 2 * RANK), F32),
            pltpu.VMEM((RANK, 2, 2 * RANK), F32),
            pltpu.VMEM((RANK * 16, 2 * RANK), F32),
            dma((NC, 2)),
            dma((3,)),
            dma((NC,)),
            dma((NC,)),
            dma((NC,)),
            dma((NC,)),
            dma(()),
            dma((NX,)),
            dma(()),
            dma((NX,)),
            dma(()),
            dma(()),
            dma(()),
            dma(()),
            pltpu.SemaphoreType.REGULAR((3,)),
        ],
        compiler_params=pltpu.CompilerParams(
            collective_id=0, has_side_effects=True, vmem_limit_bytes=56 * 1024 * 1024
        ),
    )(acts, out_grads, proj_in.T, proj_out.T, prior_cov)


def solution(mesh):
    in_specs = (
        P("seq", "tensor"),
        P("seq", "tensor"),
        P("tensor", None),
        P("tensor", None),
        P("seq", "tensor"),
    )
    return jax.shard_map(
        per_device, mesh=mesh, in_specs=in_specs, out_specs=P("seq", "tensor"), check_vma=False
    )
```

```python
import functools

import jax
import jax.numpy as jnp
from jax import lax
from jax.experimental import pallas as pl
from jax.experimental.pallas import tpu as pltpu
from jax.sharding import PartitionSpec as P

RANK = 64
LEN = 256
NZ, NX, NK, NC = 8, 4, 2, 4
MESH = pl.DeviceIdType.MESH
BF = jnp.bfloat16
F32 = jnp.float32
STOP = 9
GROUPS = (2, 1, 3, 0)


def split(v):
    hi = v.astype(BF)
    return hi, (v - hi.astype(F32)).astype(BF)


def dot_t(a, b):
    return lax.dot_general(a, b, (((1,), (1,)), ((), ())), preferred_element_type=F32)


def dot(a, b):
    return lax.dot_general(a, b, (((1,), (0,)), ((), ())), preferred_element_type=F32)


def kernel(
    acts, grads, pin, pout, prior, out,
    a_v, g_v, pi_v, po_v, prior_v, part, rsbuf, tmp, pbuf, sbuf, stage, colbuf,
    ld_sem, w_sem, rs_s, rs_r, p_s, p_r, col_s, col_r, cc_s, cc_r, met,
):
    r = lax.axis_index("seq")
    c = lax.axis_index("tensor")
    z = r // (NX * NK)
    x = (r // NK) % NX
    k = r % NK

    def seq_of(zz, xx, kk):
        return (zz * NX + xx) * NK + kk

    tok = acts.shape[0] // NC
    weights = [
        pltpu.make_async_copy(pin, pi_v, w_sem.at[0]),
        pltpu.make_async_copy(pout, po_v, w_sem.at[1]),
    ]
    prior_copy = pltpu.make_async_copy(prior, prior_v, w_sem.at[2])

    def shift(n):
        return (2 + 3 * n + 3 * (n * (n - 1) // 2)) % NC

    def rows_of(n):
        return pl.ds(pl.multiple_of(((c + shift(n)) % NC) * tok, tok), tok)

    def load_acts(n):
        return pltpu.make_async_copy(acts.at[rows_of(n)], a_v.at[n], ld_sem.at[n, 0])

    def load_grads(n):
        return pltpu.make_async_copy(grads.at[rows_of(n)], g_v.at[n], ld_sem.at[n, 1])

    weights[0].start()
    load_acts(0).start()
    weights[1].start()
    load_grads(0).start()
    load_acts(1).start()

    barrier = pltpu.get_barrier_semaphore()
    peers = [(r, (c + d) % NC) for d in range(1, NC)]
    peers += [(seq_of(z, x, 1 - k), c)]
    line = {d: (seq_of((z + d) % NZ, x, k), c) for d in (1, 2, NZ - 2, NZ - 1)}
    across = [(seq_of(z, (x + d) % NX, k), c) for d in range(1, NX)]
    peers += [line[1], line[NZ - 1]] + across

    def tell(sem, group):
        for peer in group:
            pl.semaphore_signal(sem, inc=1, device_id=peer, device_id_type=MESH)

    tell(barrier, peers)

    def remote(src, dst, s, rs, peer):
        return pltpu.make_async_remote_copy(
            src_ref=src, dst_ref=dst, send_sem=s, recv_sem=rs, device_id=peer, device_id_type=MESH
        )

    def rs_copy(n):
        dc = shift(n)
        peer = (r, (c + dc) % NC)
        return remote(part.at[n], rsbuf.at[dc], rs_s.at[dc], rs_r.at[dc], peer)

    weights[0].wait()
    weights[1].wait()

    def block(n, carry):
        load_acts(n).wait()

        @pl.when(n < NC - 1)
        def _():
            load_grads(n + 1).start()

        part[n, :, :RANK] = dot_t(a_v[n], pi_v[...])
        load_grads(n).wait()

        @pl.when(n < NC - 2)
        def _():
            load_acts(n + 2).start()

        @pl.when(n == NC - 2)
        def _():
            prior_copy.start()

        part[n, :, RANK:] = dot_t(g_v[n], po_v[...])

        @pl.when(n == 0)
        def _():
            pl.semaphore_wait(barrier, len(peers))
            tell(met.at[0], [line[1], line[NZ - 1]])

        if STOP > 0:

            @pl.when(n < NC - 1)
            def _():
                rs_copy(n).start()

        return carry

    lax.fori_loop(0, NC, block, 0)
    sends = [rs_copy(n) for n in range(NC - 1)] if STOP > 0 else []
    pl.semaphore_wait(met.at[0], 2)
    tell(met.at[1], [line[2], line[NZ - 2]])
    if STOP <= 1:
        for copy in sends:
            copy.wait()
        prior_copy.wait()
        pl.semaphore_wait(met.at[1], 2)
        out[...] = prior_v[...] + rsbuf[0, 0, 0]
        return
    for copy in sends:
        copy.wait_recv()
    both = ((part[3] + rsbuf[2]) + (rsbuf[1] + rsbuf[3])).T
    hi, lo = split(both)
    in_hi, in_lo = hi[:RANK], lo[:RANK]
    o_hi, o_lo = hi[RANK:], lo[RANK:]
    dup_hi = jnp.concatenate([in_hi, in_hi], axis=0)
    dup_lo = jnp.concatenate([in_lo, in_lo], axis=0)
    tmp[...] = dot_t(
        jnp.concatenate([o_hi, o_hi, o_lo], axis=1), jnp.concatenate([dup_hi, dup_lo, dup_hi], axis=1)
    )
    half = RANK // 2
    low = lax.broadcasted_iota(jnp.int32, (half, 2 * RANK), 1) < RANK
    pbuf[c] = jnp.where(low, tmp[pl.ds(0, half, stride=2), :], tmp[pl.ds(1, half, stride=2), :])

    p_copies = []
    for dc in (2, 1, 3):
        copy = remote(pbuf.at[c], pbuf.at[c], p_s.at[dc], p_r.at[dc], (r, (c + dc) % NC))
        copy.start()
        p_copies.append(copy)
    pl.semaphore_wait(met.at[1], 2)
    tell(met.at[2], across)
    for copy in p_copies:
        copy.wait_recv()
    pl.semaphore_wait(met.at[2], NX - 1)
    scale = 1.0 / 16.0
    s0 = (pbuf[0] + pbuf[1]) * scale
    s1 = (pbuf[2] + pbuf[3]) * scale
    sbuf[:half] = s0
    sbuf[half:] = s1

    def slot(zz, xx, kk):
        return (kk * NX + xx) * NZ + zz

    def tile(i):
        return pl.ds(pl.multiple_of(i * 8, 8), 8)

    me = slot(z, x, k)
    first, second = sbuf[tile(c), :], sbuf[tile(c + NC), :]
    for q in range(NZ * NX):
        stage[q, :8, :] = first
        stage[q, 8:16, :] = second
        stage[q, 16:17, :] = s0[q : q + 1]
        stage[q, 17:18, :] = s1[q : q + 1]
    colbuf[me, :8, :] = first
    colbuf[me, 8:16, :] = second
    colbuf[me, 16:18, :] = stage[z * NX + x, 16:18, :]
    if STOP <= 2:
        for copy in sends + p_copies:
            copy.wait_send()
        prior_copy.wait()
        out[...] = prior_v[...] + colbuf[0, 0, 0]
        return

    used = pl.ds(0, 18)

    def message(dz, dx):
        zz, xx = (z + dz) % NZ, (x + dx) % NX
        src, dst = stage.at[zz * NX + xx, used], colbuf.at[me, used]
        return remote(src, dst, col_s, col_r.at[dx], (seq_of(zz, xx, k), c))

    sibling = (seq_of(z, x, 1 - k), c)

    def group(xx, count):
        return colbuf.at[pl.ds(slot(0, xx, k), count), used]

    def send(t, carry):
        dx, j = shift(t // NZ), t % NZ
        dz = NZ // 2 + (1 - 2 * (j % 2)) * ((j + 1) // 2)
        message(dz, dx).start()
        return carry

    lax.fori_loop(0, NZ * NX - 1, send, 0)
    for dx in GROUPS:
        count = NZ if dx else NZ - 1
        xx = (x - dx) % NX
        got = group(xx, count)
        pltpu.make_async_copy(got, got, col_r.at[dx]).wait()
        whole = group(xx, NZ)
        remote(whole, whole, cc_s, cc_r, sibling).start()

    total = NZ * NX
    mine = colbuf.at[pl.ds(0, total), used]
    prior_copy.wait()
    pltpu.make_async_copy(mine, mine, cc_r).wait()
    flat = colbuf.reshape(RANK * 24, 2 * RANK)
    even = (jnp.zeros((NZ * NX * NK, 2 * RANK), jnp.int32) + k) == 0
    parts = []
    for h in range(2):
        v = flat[pl.ds(16 + h, 64, stride=24), :]
        parts.append(jnp.where(even, v, pltpu.roll(v, RANK, 1)))
    lhs = jnp.concatenate(parts, axis=0).T[:RANK]
    l_hi, l_lo = split(lhs)
    l_all = jnp.concatenate([l_hi, l_hi, l_lo], axis=1)
    for p in range(0, 8, 2):
        block = jnp.concatenate(
            [
                jnp.concatenate([flat[pl.ds(8 * h + q, 64, stride=24), :] for h in range(2)], axis=0)
                for q in (p, p + 1)
            ],
            axis=1,
        )
        b_hi, b_lo = split(block)
        product = dot(l_all, jnp.concatenate([b_hi, b_lo, b_hi], axis=0))
        cols = slice(128 * p, 128 * p + 256)
        out[:, cols] = prior_v[:, cols] + product * (1.0 / 128.0)

    for copy in sends + p_copies:
        copy.wait_send()
    others = colbuf.at[pl.ds(0, total - 1), used]
    pltpu.make_async_copy(others, others, col_s).wait()
    pltpu.make_async_copy(mine, mine, cc_s).wait()


def per_device(acts, out_grads, proj_in, proj_out, prior_cov):
    tokens, ff = acts.shape
    d = out_grads.shape[1]
    tok = tokens // NC
    hbm = pl.BlockSpec(memory_space=pl.ANY)
    dma = pltpu.SemaphoreType.DMA
    return pl.pallas_call(
        kernel,
        out_shape=pltpu.VMEM(prior_cov.shape, F32),
        in_specs=[hbm] * 5,
        out_specs=pl.BlockSpec(memory_space=pltpu.VMEM),
        scratch_shapes=[
            pltpu.VMEM((NC, tok, ff), BF),
            pltpu.VMEM((NC, tok, d), BF),
            pltpu.VMEM((RANK, ff), BF),
            pltpu.VMEM((RANK, d), BF),
            pltpu.VMEM(prior_cov.shape, F32),
            pltpu.VMEM((NC, tok, 2 * RANK), F32),
            pltpu.VMEM((NC, tok, 2 * RANK), F32),
            pltpu.VMEM((RANK, 2 * RANK), F32),
            pltpu.VMEM((NC, RANK // 2, 2 * RANK), F32),
            pltpu.VMEM((RANK, 2 * RANK), F32),
            pltpu.VMEM((NZ * NX, 24, 2 * RANK), F32),
            pltpu.VMEM((RANK, 24, 2 * RANK), F32),
            dma((NC, 2)),
            dma((3,)),
            dma((NC,)),
            dma((NC,)),
            dma((NC,)),
            dma((NC,)),
            dma(()),
            dma((NX,)),
            dma(()),
            dma(()),
            pltpu.SemaphoreType.REGULAR((3,)),
        ],
        compiler_params=pltpu.CompilerParams(
            collective_id=0, has_side_effects=True, vmem_limit_bytes=56 * 1024 * 1024
        ),
    )(acts, out_grads, proj_in.T, proj_out.T, prior_cov)


def solution(mesh):
    in_specs = (
        P("seq", "tensor"),
        P("seq", "tensor"),
        P("tensor", None),
        P("tensor", None),
        P("seq", "tensor"),
    )
    return jax.shard_map(
        per_device, mesh=mesh, in_specs=in_specs, out_specs=P("seq", "tensor"), check_vma=False
    )
```

```python
import functools

import jax
import jax.numpy as jnp
from jax import lax
from jax.experimental import pallas as pl
from jax.experimental.pallas import tpu as pltpu
from jax.sharding import PartitionSpec as P

RANK = 64
LEN = 256
NZ, NX, NK, NC = 8, 4, 2, 4
MESH = pl.DeviceIdType.MESH
BF = jnp.bfloat16
F32 = jnp.float32
STOP = 9
GROUPS = (2, 1, 3, 0)


def split(v):
    hi = v.astype(BF)
    return hi, (v - hi.astype(F32)).astype(BF)


def dot_t(a, b):
    return lax.dot_general(a, b, (((1,), (1,)), ((), ())), preferred_element_type=F32)


def dot(a, b):
    return lax.dot_general(a, b, (((1,), (0,)), ((), ())), preferred_element_type=F32)


def kernel(
    acts, grads, pin, pout, prior, out,
    a_v, g_v, pi_v, po_v, prior_v, part, rsbuf, tmp, pbuf, sbuf, stage, colbuf,
    ld_sem, w_sem, rs_s, rs_r, p_s, p_r, col_s, col_r, cc_s, cc_r, met,
):
    r = lax.axis_index("seq")
    c = lax.axis_index("tensor")
    z = r // (NX * NK)
    x = (r // NK) % NX
    k = r % NK

    def seq_of(zz, xx, kk):
        return (zz * NX + xx) * NK + kk

    tok = acts.shape[0] // NC
    weights = [
        pltpu.make_async_copy(pin, pi_v, w_sem.at[0]),
        pltpu.make_async_copy(pout, po_v, w_sem.at[1]),
    ]
    prior_copy = pltpu.make_async_copy(prior, prior_v, w_sem.at[2])

    def shift(n):
        return (2 + 3 * n + 3 * (n * (n - 1) // 2)) % NC

    def rows_of(n):
        return pl.ds(pl.multiple_of(((c + shift(n)) % NC) * tok, tok), tok)

    def load_acts(n):
        return pltpu.make_async_copy(acts.at[rows_of(n)], a_v.at[n], ld_sem.at[n, 0])

    def load_grads(n):
        return pltpu.make_async_copy(grads.at[rows_of(n)], g_v.at[n], ld_sem.at[n, 1])


    barrier = pltpu.get_barrier_semaphore()
    peers = [(r, (c + d) % NC) for d in range(1, NC)]
    peers += [(seq_of(z, x, 1 - k), c)]
    line = {d: (seq_of((z + d) % NZ, x, k), c) for d in (1, 2, NZ - 2, NZ - 1)}
    across = [(seq_of(z, (x + d) % NX, k), c) for d in range(1, NX)]
    peers += [line[1], line[NZ - 1]] + across

    def tell(sem, group):
        for peer in group:
            pl.semaphore_signal(sem, inc=1, device_id=peer, device_id_type=MESH)

    tell(barrier, peers)
    weights[0].start()
    load_acts(0).start()
    weights[1].start()
    load_grads(0).start()
    load_acts(1).start()

    def remote(src, dst, s, rs, peer):
        return pltpu.make_async_remote_copy(
            src_ref=src, dst_ref=dst, send_sem=s, recv_sem=rs, device_id=peer, device_id_type=MESH
        )

    def rs_copy(n):
        dc = shift(n)
        peer = (r, (c + dc) % NC)
        return remote(part.at[n], rsbuf.at[dc], rs_s.at[dc], rs_r.at[dc], peer)

    weights[0].wait()
    weights[1].wait()

    def block(n, carry):
        load_acts(n).wait()

        @pl.when(n < NC - 1)
        def _():
            load_grads(n + 1).start()

        part[n, :, :RANK] = dot_t(a_v[n], pi_v[...])
        load_grads(n).wait()

        @pl.when(n < NC - 2)
        def _():
            load_acts(n + 2).start()

        @pl.when(n == NC - 2)
        def _():
            prior_copy.start()

        part[n, :, RANK:] = dot_t(g_v[n], po_v[...])

        @pl.when(n == 0)
        def _():
            pl.semaphore_wait(barrier, len(peers))
            tell(met.at[0], [line[1], line[NZ - 1]])

        if STOP > 0:

            @pl.when(n < NC - 1)
            def _():
                rs_copy(n).start()

        return carry

    lax.fori_loop(0, NC, block, 0)
    sends = [rs_copy(n) for n in range(NC - 1)] if STOP > 0 else []
    pl.semaphore_wait(met.at[0], 2)
    tell(met.at[1], [line[2], line[NZ - 2]])
    if STOP <= 1:
        for copy in sends:
            copy.wait()
        prior_copy.wait()
        pl.semaphore_wait(met.at[1], 2)
        out[...] = prior_v[...] + rsbuf[0, 0, 0]
        return
    for copy in sends:
        copy.wait_recv()
    both = ((part[3] + rsbuf[2]) + (rsbuf[1] + rsbuf[3])).T
    hi, lo = split(both)
    in_hi, in_lo = hi[:RANK], lo[:RANK]
    o_hi, o_lo = hi[RANK:], lo[RANK:]
    dup_hi = jnp.concatenate([in_hi, in_hi], axis=0)
    dup_lo = jnp.concatenate([in_lo, in_lo], axis=0)
    tmp[...] = dot_t(
        jnp.concatenate([o_hi, o_hi, o_lo], axis=1), jnp.concatenate([dup_hi, dup_lo, dup_hi], axis=1)
    )
    half = RANK // 2
    low = lax.broadcasted_iota(jnp.int32, (half, 2 * RANK), 1) < RANK
    pbuf[c] = jnp.where(low, tmp[pl.ds(0, half, stride=2), :], tmp[pl.ds(1, half, stride=2), :])

    p_copies = []
    for dc in (2, 1, 3):
        copy = remote(pbuf.at[c], pbuf.at[c], p_s.at[dc], p_r.at[dc], (r, (c + dc) % NC))
        copy.start()
        p_copies.append(copy)
    pl.semaphore_wait(met.at[1], 2)
    tell(met.at[2], across)
    for copy in p_copies:
        copy.wait_recv()
    pl.semaphore_wait(met.at[2], NX - 1)
    scale = 1.0 / 16.0
    s0 = (pbuf[0] + pbuf[1]) * scale
    s1 = (pbuf[2] + pbuf[3]) * scale
    sbuf[:half] = s0
    sbuf[half:] = s1

    def slot(zz, xx, kk):
        return (kk * NX + xx) * NZ + zz

    def tile(i):
        return pl.ds(pl.multiple_of(i * 8, 8), 8)

    me = slot(z, x, k)
    first, second = sbuf[tile(c), :], sbuf[tile(c + NC), :]
    for q in range(NZ * NX):
        stage[q, :8, :] = first
        stage[q, 8:16, :] = second
        stage[q, 16:17, :] = s0[q : q + 1]
        stage[q, 17:18, :] = s1[q : q + 1]
    colbuf[me, :8, :] = first
    colbuf[me, 8:16, :] = second
    colbuf[me, 16:18, :] = stage[z * NX + x, 16:18, :]
    if STOP <= 2:
        for copy in sends + p_copies:
            copy.wait_send()
        prior_copy.wait()
        out[...] = prior_v[...] + colbuf[0, 0, 0]
        return

    used = pl.ds(0, 18)

    def message(dz, dx):
        zz, xx = (z + dz) % NZ, (x + dx) % NX
        src, dst = stage.at[zz * NX + xx, used], colbuf.at[me, used]
        return remote(src, dst, col_s, col_r.at[dx], (seq_of(zz, xx, k), c))

    sibling = (seq_of(z, x, 1 - k), c)

    def group(xx, count):
        return colbuf.at[pl.ds(slot(0, xx, k), count), used]

    def send(t, carry):
        dx, j = shift(t // NZ), t % NZ
        dz = NZ // 2 + (1 - 2 * (j % 2)) * ((j + 1) // 2)
        message(dz, dx).start()
        return carry

    lax.fori_loop(0, NZ * NX - 1, send, 0)
    for dx in GROUPS:
        count = NZ if dx else NZ - 1
        xx = (x - dx) % NX
        got = group(xx, count)
        pltpu.make_async_copy(got, got, col_r.at[dx]).wait()
        whole = group(xx, NZ)
        remote(whole, whole, cc_s, cc_r, sibling).start()

    total = NZ * NX
    mine = colbuf.at[pl.ds(0, total), used]
    prior_copy.wait()
    pltpu.make_async_copy(mine, mine, cc_r).wait()
    flat = colbuf.reshape(RANK * 24, 2 * RANK)
    even = (jnp.zeros((NZ * NX * NK, 2 * RANK), jnp.int32) + k) == 0
    parts = []
    for h in range(2):
        v = flat[pl.ds(16 + h, 64, stride=24), :]
        parts.append(jnp.where(even, v, pltpu.roll(v, RANK, 1)))
    lhs = jnp.concatenate(parts, axis=0).T[:RANK]
    l_hi, l_lo = split(lhs)
    l_all = jnp.concatenate([l_hi, l_hi, l_lo], axis=1)
    for p in range(0, 8, 2):
        block = jnp.concatenate(
            [
                jnp.concatenate([flat[pl.ds(8 * h + q, 64, stride=24), :] for h in range(2)], axis=0)
                for q in (p, p + 1)
            ],
            axis=1,
        )
        b_hi, b_lo = split(block)
        product = dot(l_all, jnp.concatenate([b_hi, b_lo, b_hi], axis=0))
        cols = slice(128 * p, 128 * p + 256)
        out[:, cols] = prior_v[:, cols] + product * (1.0 / 128.0)

    for copy in sends + p_copies:
        copy.wait_send()
    others = colbuf.at[pl.ds(0, total - 1), used]
    pltpu.make_async_copy(others, others, col_s).wait()
    pltpu.make_async_copy(mine, mine, cc_s).wait()


def per_device(acts, out_grads, proj_in, proj_out, prior_cov):
    tokens, ff = acts.shape
    d = out_grads.shape[1]
    tok = tokens // NC
    hbm = pl.BlockSpec(memory_space=pl.ANY)
    dma = pltpu.SemaphoreType.DMA
    return pl.pallas_call(
        kernel,
        out_shape=pltpu.VMEM(prior_cov.shape, F32),
        in_specs=[hbm] * 5,
        out_specs=pl.BlockSpec(memory_space=pltpu.VMEM),
        scratch_shapes=[
            pltpu.VMEM((NC, tok, ff), BF),
            pltpu.VMEM((NC, tok, d), BF),
            pltpu.VMEM((RANK, ff), BF),
            pltpu.VMEM((RANK, d), BF),
            pltpu.VMEM(prior_cov.shape, F32),
            pltpu.VMEM((NC, tok, 2 * RANK), F32),
            pltpu.VMEM((NC, tok, 2 * RANK), F32),
            pltpu.VMEM((RANK, 2 * RANK), F32),
            pltpu.VMEM((NC, RANK // 2, 2 * RANK), F32),
            pltpu.VMEM((RANK, 2 * RANK), F32),
            pltpu.VMEM((NZ * NX, 24, 2 * RANK), F32),
            pltpu.VMEM((RANK, 24, 2 * RANK), F32),
            dma((NC, 2)),
            dma((3,)),
            dma((NC,)),
            dma((NC,)),
            dma((NC,)),
            dma((NC,)),
            dma(()),
            dma((NX,)),
            dma(()),
            dma(()),
            pltpu.SemaphoreType.REGULAR((3,)),
        ],
        compiler_params=pltpu.CompilerParams(
            collective_id=0, has_side_effects=True, vmem_limit_bytes=56 * 1024 * 1024
        ),
    )(acts, out_grads, proj_in.T, proj_out.T, prior_cov)


def solution(mesh):
    in_specs = (
        P("seq", "tensor"),
        P("seq", "tensor"),
        P("tensor", None),
        P("tensor", None),
        P("seq", "tensor"),
    )
    return jax.shard_map(
        per_device, mesh=mesh, in_specs=in_specs, out_specs=P("seq", "tensor"), check_vma=False
    )
```
